128 devices in a mesh: group: 2 (over x_lo), shard: 64 (over z, x_hi, y, core).
Axes of the slice: x: 4 (x_hi: 2, x_lo: 2; x = x_hi * 2 + x_lo), y: 4, z: 4, core: 2. Of those that a mesh axis runs over, the one named last changes fastest.
Arguments:
- replica_weights: bfloat16 [2, 64, 512, 2048], P('group', None, 'shard'), may hold values from -6 to 6
- anchor_slabs: float32 [64, 2, 512, 2048], P('shard', None, None, 'group'), may hold values from -6 to 6
- momentum_slabs: float32 [64, 2, 512, 2048], P('shard', None, None, 'group'), may hold values from -4 to 4
- slab_owner: int32 [64], replicated, may hold values from 0 to 63, as said below
- replica_embed: bfloat16 [2, 768, 512], P('group', 'shard'), may hold values from -6 to 6
- anchor_embed: float32 [768, 512], P('shard'), may hold values from -6 to 6
- momentum_embed: float32 [768, 512], P('shard'), may hold values from -4 to 4
- embed_basis: float32 [768, 64], P('shard'), may hold values from -0.21875 to 0.21875
Outputs:
- new_anchor_slabs: float32 [64, 2, 512, 2048], P('shard', None, None, 'group')
- new_momentum_slabs: float32 [64, 2, 512, 2048], P('shard', None, None, 'group')
- new_weights: bfloat16 [2, 64, 512, 2048], P('group', None, 'shard')
- new_anchor_embed: float32 [768, 512], P('shard')
- new_momentum_embed: float32 [768, 512], P('shard')
- new_embed_weights: bfloat16 [2, 768, 512], P('group', 'shard')
The draws below stay inside these ranges and needn't reach their ends.
Inputs may be any that keep to these rules, and one draw needn't show every extreme that they name: `slab_owner`: of the devices of shard, a quarter own 2 matrices each, half own 1 each and a quarter own none.
All inputs are finite; a program needn't handle non-finite values.
Results may differ from the reference program's by a relative error of at most 0.008.
Values may be sent and summed in bfloat16 or wider, within the bound.
A program may use at most 128 MiB of HBM per device.

```python
import jax
import jax.numpy as jnp
from jax import lax

D = 512
FF = 2048
PATCH = 768
RANK = 64
SLABS_DEV = 1
CAP = 2
NSLAB = 64
N_GROUP = 2
N_SHARD = 64


def draw_slab_owner(key, part):
    devices = NSLAB // SLABS_DEV
    quarter = devices // 4
    order_key = jax.random.fold_in(key, 11)
    shuffle_key = jax.random.fold_in(key, 23)
    device_order = jax.random.permutation(order_key, devices).astype(jnp.int32)
    heavy_owners = jnp.repeat(device_order[:quarter], CAP)
    middle_owners = jnp.repeat(device_order[quarter:3 * quarter], SLABS_DEV)
    owners = jnp.concatenate([heavy_owners, middle_owners]).astype(jnp.int32)
    slab_order = jax.random.permutation(shuffle_key, NSLAB).astype(jnp.int32)
    return jnp.take(owners, slab_order).astype(jnp.int32)


def levels(own_key, shape, cuts, smallest, largest):
    def one(dim, parts):
        draws = jax.random.uniform(jax.random.fold_in(jax.random.fold_in(own_key, 6), dim), (parts,), jnp.float32, smallest / len(cuts), largest / len(cuts))
        return jnp.repeat(jnp.exp(draws), shape[dim] // parts).reshape((-1,) + (1,) * (len(shape) - dim - 1))

    gain = one(*cuts[0])
    for cut in cuts[1:]:
        gain = gain * one(*cut)
    return gain


def bell_draw(stream_key, dims, deviation, most, shards=(), kind=jnp.bfloat16):
    array = deviation * jax.random.normal(stream_key, dims, jnp.float32)
    if shards:
        array = array * levels(stream_key, dims, shards, -0.22, 0.18)
    return jnp.clip(array, -most, most).astype(kind)


def setup_inputs(seed: int = 0) -> dict:
    seeds = jax.random.split(jax.random.key(seed), 9)
    return {
        "replica_weights": bell_draw(seeds[0], (N_GROUP, NSLAB, D, FF), 1.0, 6.0, ((0, 2), (2, 64))),
        "anchor_slabs": bell_draw(seeds[1], (N_SHARD, CAP, D, FF), 1.0, 6.0, ((0, 64), (3, 2)), jnp.float32),
        "momentum_slabs": bell_draw(seeds[2], (N_SHARD, CAP, D, FF), 0.5, 4.0, ((0, 64), (3, 2)), jnp.float32),
        "slab_owner": draw_slab_owner(jax.random.fold_in(seeds[8], 71), 0),
        "replica_embed": bell_draw(seeds[4], (N_GROUP, PATCH, D), 1.0, 6.0, ((0, 2), (1, 64))),
        "anchor_embed": bell_draw(seeds[5], (PATCH, D), 1.0, 6.0, ((0, 64),), jnp.float32),
        "momentum_embed": bell_draw(seeds[6], (PATCH, D), 0.5, 4.0, ((0, 64),), jnp.float32),
        "embed_basis": bell_draw(seeds[7], (PATCH, RANK), PATCH ** -0.5, 0.21875, ((0, 64),), jnp.float32),
    }


OUTER_RATE = 0.7
MOMENTUM_COEF = 0.9


def slot_tables(slab_owner, devices, capacity):
    slab_count = slab_owner.shape[0]
    order_ids = jnp.arange(slab_count, dtype=jnp.int32)
    same_owner = slab_owner[:, None] == slab_owner[None, :]
    earlier = order_ids[None, :] < order_ids[:, None]
    slot_index = jnp.sum((same_owner & earlier).astype(jnp.int32), axis=1).astype(jnp.int32)
    matches = (slab_owner[:, None, None] == jnp.arange(devices, dtype=jnp.int32)[None, :, None]) & (slot_index[:, None, None] == jnp.arange(capacity, dtype=jnp.int32)[None, None, :])
    slab_of = jnp.sum(jnp.where(matches, order_ids[:, None, None], 0), axis=0).astype(jnp.int32)
    slot_used = jnp.any(matches, axis=0)
    return slot_index, slab_of, slot_used


def nesterov(anchor_value, moment, mean_value):
    outer_grad = anchor_value - mean_value
    new_moment = MOMENTUM_COEF * moment + outer_grad
    new_anchor = anchor_value - OUTER_RATE * (outer_grad + MOMENTUM_COEF * new_moment)
    return new_anchor, new_moment


def reference(replica_weights, anchor_slabs, momentum_slabs, slab_owner, replica_embed, anchor_embed, momentum_embed, embed_basis):
    devices = anchor_slabs.shape[0]
    capacity = anchor_slabs.shape[1]
    slot_index, slab_of, slot_used = slot_tables(slab_owner, devices, capacity)

    def per_device(items):
        anchor_here, moment_here, slab_ids, used_here = items
        picked = jnp.take(replica_weights, slab_ids, axis=1).astype(jnp.float32)
        mean_rows = jnp.sum(picked, axis=0) / N_GROUP
        new_anchor, new_moment = nesterov(anchor_here, moment_here, mean_rows)
        keep = used_here[:, None, None]
        return jnp.where(keep, new_anchor, anchor_here), jnp.where(keep, new_moment, moment_here)

    new_anchor_slabs, new_momentum_slabs = lax.map(per_device, (anchor_slabs, momentum_slabs, slab_of, slot_used))
    chosen = new_anchor_slabs[slab_owner, slot_index].astype(jnp.bfloat16)
    new_weights = jnp.broadcast_to(chosen[None], (N_GROUP,) + chosen.shape)

    mean_embed = jnp.sum(replica_embed.astype(jnp.float32), axis=0) / N_GROUP
    embed_factor = jnp.dot(embed_basis.T, anchor_embed - mean_embed, precision=lax.Precision.HIGHEST)
    embed_grad = jnp.dot(embed_basis, embed_factor, precision=lax.Precision.HIGHEST)
    new_anchor_embed, new_momentum_embed = nesterov(anchor_embed, momentum_embed, anchor_embed - embed_grad)
    embed_cast = new_anchor_embed.astype(jnp.bfloat16)
    new_embed_weights = jnp.broadcast_to(embed_cast[None], (N_GROUP,) + embed_cast.shape)
    return new_anchor_slabs, new_momentum_slabs, new_weights, new_anchor_embed, new_momentum_embed, new_embed_weights
```

```python
import jax
import jax.numpy as jnp
from jax import lax
from jax.sharding import PartitionSpec as P

OUTER_RATE = 0.7
MOMENTUM_COEF = 0.9


def slot_tables(slab_owner, devices, capacity):
    slab_count = slab_owner.shape[0]
    order_ids = jnp.arange(slab_count, dtype=jnp.int32)
    same_owner = slab_owner[:, None] == slab_owner[None, :]
    earlier = order_ids[None, :] < order_ids[:, None]
    slot_index = jnp.sum((same_owner & earlier).astype(jnp.int32), axis=1)
    matches = (slab_owner[:, None, None] == jnp.arange(devices, dtype=jnp.int32)[None, :, None]) & (
        slot_index[:, None, None] == jnp.arange(capacity, dtype=jnp.int32)[None, None, :]
    )
    slab_of = jnp.sum(jnp.where(matches, order_ids[:, None, None], 0), axis=0)
    slot_used = jnp.any(matches, axis=0)
    return (slot_index, slab_of, slot_used)


def nesterov(anchor_value, moment, mean_value):
    outer_grad = anchor_value - mean_value
    new_moment = MOMENTUM_COEF * moment + outer_grad
    new_anchor = anchor_value - OUTER_RATE * (outer_grad + MOMENTUM_COEF * new_moment)
    return (new_anchor, new_moment)


def on_device(
    replica_weights,
    anchor_slabs,
    momentum_slabs,
    slab_owner,
    replica_embed,
    anchor_embed,
    momentum_embed,
    embed_basis,
):
    local_rows = replica_weights[0]
    row_count = local_rows.shape[1]
    devices = lax.axis_size("shard")
    n_group = lax.axis_size("group")
    capacity = anchor_slabs.shape[1]
    slot_index, slab_of, slot_used = slot_tables(slab_owner, devices, capacity)
    send_ids = slab_of.T.reshape(-1)
    back_ids = slot_index * devices + slab_owner
    owner_here = lax.axis_index("shard")
    my_used = lax.dynamic_index_in_dim(slot_used, owner_here, 0, keepdims=False)
    anchor_here = anchor_slabs[0]
    moment_here = momentum_slabs[0]
    summed_rows = lax.psum_scatter(local_rows, "group", scatter_dimension=2, tiled=True)
    half = summed_rows.shape[2]
    picked = jnp.take(summed_rows, send_ids, axis=0)
    picked = picked.reshape(capacity, devices, row_count, half)
    received = lax.all_to_all(picked, "shard", split_axis=1, concat_axis=1, tiled=True)
    summed = received.reshape(capacity, devices * row_count, half).astype(jnp.float32)
    new_anchor, new_moment = nesterov(anchor_here, moment_here, summed / n_group)
    keep = my_used[:, None, None]
    new_anchor = jnp.where(keep, new_anchor, anchor_here)
    new_moment = jnp.where(keep, new_moment, moment_here)
    new_half = new_anchor.astype(jnp.bfloat16)
    split_rows = new_half.reshape(capacity, devices, row_count, half)
    received = lax.all_to_all(split_rows, "shard", split_axis=1, concat_axis=1, tiled=True)
    flat_rows = received.reshape(capacity * devices, row_count, half)
    half_rows = jnp.take(flat_rows, back_ids, axis=0)
    new_rows = lax.all_gather(half_rows, "group", axis=2, tiled=True)
    embed_here = replica_embed[0].astype(jnp.float32)
    partial_factor = jnp.dot(
        embed_basis.T,
        anchor_embed / n_group - embed_here / n_group,
        precision=lax.Precision.HIGHEST,
    )
    embed_factor = lax.psum(partial_factor, ("group", "shard"))
    embed_grad = jnp.dot(embed_basis, embed_factor, precision=lax.Precision.HIGHEST)
    new_anchor_embed, new_momentum_embed = nesterov(
        anchor_embed, momentum_embed, anchor_embed - embed_grad
    )
    new_embed_rows = new_anchor_embed.astype(jnp.bfloat16)
    return (
        new_anchor[None],
        new_moment[None],
        new_rows[None],
        new_anchor_embed,
        new_momentum_embed,
        new_embed_rows[None],
    )


def solution(mesh):
    in_specs = (
        P("group", None, "shard", None),
        P("shard", None, None, "group"),
        P("shard", None, None, "group"),
        P(),
        P("group", "shard", None),
        P("shard", None),
        P("shard", None),
        P("shard", None),
    )
    out_specs = (
        P("shard", None, None, "group"),
        P("shard", None, None, "group"),
        P("group", None, "shard", None),
        P("shard", None),
        P("shard", None),
        P("group", "shard", None),
    )
    return jax.shard_map(
        on_device, mesh=mesh, in_specs=in_specs, out_specs=out_specs, check_vma=False
    )
```

```python
import functools

import jax
import jax.numpy as jnp
from jax import lax
from jax.experimental import pallas as pl
from jax.experimental.pallas import tpu as pltpu
from jax.sharding import PartitionSpec as P

OUTER_RATE = 0.7
MOMENTUM_COEF = 0.9
GRAD_COEF = OUTER_RATE * (1.0 + MOMENTUM_COEF)
MOMENT_COEF = OUTER_RATE * MOMENTUM_COEF * MOMENTUM_COEF
PLANES = 2
INNER = {64: 8, 8: 2}
CHUNKS = 4
UNROLL = 4
MESH = pl.DeviceIdType.MESH


def place(shard, inner):
    plane = lax.rem(lax.div(shard, inner), PLANES)
    spot = lax.div(shard, PLANES * inner) * inner + lax.rem(shard, inner)
    return plane, spot


def shard_of(spot, plane, inner):
    return lax.div(spot, inner) * (PLANES * inner) + plane * inner + lax.rem(spot, inner)


def loop(count, body):
    unroll = UNROLL if count % UNROLL == 0 else 1

    def step(i, carry):
        for u in range(unroll):
            body(i * unroll + u)
        return carry

    lax.fori_loop(0, count // unroll, step, 0)


def each(start, stop, body):
    def step(i, carry):
        body(i)
        return carry

    lax.fori_loop(start, stop, step, 0)


def route_kernel(sizes, tabs, xs, xo, q, part, n_out, nr_out, f_out, e_out, *scratch):
    shards, slabs, slots, ranks, inner, width = sizes
    chunks = CHUNKS
    spots = shards // PLANES
    (r, s, fc, cf, ys, qr, qc, qd, nn) = [scratch[i * chunks : (i + 1) * chunks] for i in range(9)]
    er, e1, ex, e2, *sems = scratch[9 * chunks :]
    (sa, ra, sc, rc, sq, rq, sd, rd, sf, sn, lo) = sems[:11]
    (rf, rn, se, re, sx, rx, sg, rg, le) = sems[11:]

    group = lax.axis_index("group")
    shard = lax.axis_index("shard")
    plane, spot = place(shard, inner)
    line, lane = lax.div(spot, inner), lax.rem(spot, inner)
    other = 1 - plane
    partner = (1 - group, shard)
    across = (1 - group, shard_of(spot, other, inner))
    corner = (group, shard_of(spot, other, inner))

    def peer(i):
        d = lax.rem(spot + i, spots)
        return d, (group, shard_of(d, plane, inner))

    def remote(src, dst, send, recv, device):
        return pltpu.make_async_remote_copy(
            src_ref=src, dst_ref=dst, send_sem=send, recv_sem=recv, device_id=device, device_id_type=MESH
        )

    def drain(ref, sem):
        pltpu.make_async_copy(ref, ref, sem).wait()

    off_fo, off_rk = 0, slots
    off_fc, off_fp = 2 * slots, 2 * slots + ranks
    off_in, off_ts = 2 * slots + 2 * ranks, 2 * slots + 2 * ranks + slabs

    barrier = pltpu.get_barrier_semaphore()

    def greet(i):
        pl.semaphore_signal(barrier, inc=1, device_id=peer(i)[1], device_id_type=MESH)

    each(1, spots, greet)
    for device in (partner, across, corner):
        pl.semaphore_signal(barrier, inc=1, device_id=device, device_id_type=MESH)
    pl.semaphore_wait(barrier, spots - 1 + 3)

    def cols(k):
        return pl.ds(k * width, width)

    for k in range(chunks):
        remote(xs.at[:, :, cols(k)], r[k], sa.at[k], ra.at[k], partner).start()

    def send_part(i):
        d, device = peer(i)
        remote(part.at[d], er.at[spot], se, re, device).start()

    each(1, spots, send_part)
    er[spot] = part[spot]

    for k in range(chunks):

        def send_q(i, k=k):
            d, device = peer(i)
            remote(
                q.at[:, lax.div(d, inner), :, lax.rem(d, inner), :, cols(k)], qr[k].at[spot], sq.at[k], rq.at[k], device
            ).start()

        each(1, spots, send_q)
        pltpu.make_async_copy(q.at[:, line, :, lane, :, cols(k)], qr[k].at[spot], lo.at[k]).start()

    def stage_sum(k):
        drain(r[k], ra.at[k])

        def add(t):
            both = xo[t, :, cols(k)].astype(jnp.float32) + r[k][t].astype(jnp.float32)
            s[k][t] = both.astype(jnp.bfloat16)

        loop(slabs, add)

        def pick_cross(i):
            fc[k][i] = s[k][tabs[off_fc + i]]

        loop(ranks, pick_cross)
        remote(fc[k], cf[k], sc.at[k], rc.at[k], across).start()

        def pick_own(j):
            ys[k][lax.div(j, 2), lax.rem(j, 2), plane] = s[k][tabs[off_fo + j]]

        loop(slots, pick_own)

    def stage_q(k):
        drain(qr[k].at[pl.ds(0, spots - 1)], rq.at[k])
        drain(qr[k].at[0], lo.at[k])

        def pick(i):
            j = tabs[off_fp + i]
            qc[k][i] = qr[k][lax.div(j, 2), lax.rem(j, 2), other]

        loop(ranks, pick)
        remote(qc[k], qd[k], sd.at[k], rd.at[k], across).start()

    def stage_route(k):
        drain(cf[k], rc.at[k])

        def pick(j):
            ys[k][lax.div(j, 2), lax.rem(j, 2), other] = cf[k][tabs[off_rk + j]]

        loop(slots, pick)

        def send(i):
            d, device = peer(i)
            remote(ys[k].at[d], f_out.at[:, line, :, lane, :, cols(k)], sf.at[k], rf.at[k], device).start()

        each(1, spots, send)
        pltpu.make_async_copy(ys[k].at[spot], f_out.at[:, line, :, lane, :, cols(k)], lo.at[chunks + k]).start()

    def stage_new(k):
        drain(qd[k], rd.at[k])

        def combine(t):
            own = tabs[off_in + t]
            where = tabs[off_ts + t]
            j = where * own
            here = qr[k][lax.div(j, 2), lax.rem(j, 2), plane]
            there = qd[k][where * (1 - own)]
            base = jnp.where(own == 1, here.astype(jnp.float32), there.astype(jnp.float32))
            new = base + (0.5 * GRAD_COEF) * s[k][t].astype(jnp.float32)
            nn[k][t] = new.astype(jnp.bfloat16)

        loop(slabs, combine)
        remote(nn[k], nr_out.at[:, :, cols(k)], sn.at[k], rn.at[k], partner).start()
        pltpu.make_async_copy(nn[k], n_out.at[:, :, cols(k)], lo.at[2 * chunks + k]).start()

    def factor_sum():
        drain(er.at[pl.ds(0, spots - 1)], re)
        e1[...] = jnp.sum(er[...], axis=0)
        at = PLANES * plane + group
        ex[at] = e1[...]
        for n, device in enumerate((partner, across, corner)):
            remote(e1, ex.at[at], sx.at[n], rx.at[n], device).start()

    def factor_send():
        for n in range(3):
            drain(e1, rx.at[n])
        e2[...] = jnp.sum(ex[...], axis=0)

        def send(i):
            remote(e2, e_out.at[spot], sg, rg, peer(i)[1]).start()

        each(1, spots, send)
        pltpu.make_async_copy(e2, e_out.at[spot], le).start()

    for k in range(chunks):
        stage_sum(k)
        stage_q(k)
        if k == 0:
            factor_sum()
        if k == 1:
            factor_send()
        if k >= 1:
            stage_route(k - 1)
            stage_new(k - 1)
    stage_route(chunks - 1)
    stage_new(chunks - 1)

    for k in range(chunks):
        some = qr[k].at[pl.ds(0, spots - 1)]
        drain(r[k], sa.at[k])
        drain(cf[k], sc.at[k])
        drain(qd[k], sd.at[k])
        drain(some, sq.at[k])
        drain(some, sf.at[k])
        drain(nn[k], sn.at[k])
        drain(qr[k].at[0], lo.at[chunks + k])
        drain(nn[k], lo.at[2 * chunks + k])
        drain(some, rf.at[k])
        drain(nn[k], rn.at[k])
    for n in range(3):
        drain(e1, sx.at[n])
    drain(er.at[pl.ds(0, spots - 1)], se)
    drain(er.at[pl.ds(0, spots - 1)], sg)
    drain(er.at[pl.ds(0, spots - 1)], rg)
    drain(e2, le)


def route(tabs, xs, xo, q, part):
    slabs, rows, half = xs.shape
    slots_dev, lines, _, inner, _, _ = q.shape
    shards = lines * PLANES * inner
    spots = shards // PLANES
    slots = spots * slots_dev
    ranks = slabs * 3 // 4
    width = half // CHUNKS
    vmem = lambda *shape: [pltpu.VMEM(shape, jnp.bfloat16)] * CHUNKS
    sem = pltpu.SemaphoreType.DMA
    scratch = (
        vmem(slabs, rows, width)
        + vmem(slabs, rows, width)
        + vmem(ranks, rows, width)
        + vmem(ranks, rows, width)
        + vmem(spots, slots_dev, PLANES, rows, width)
        + vmem(spots, slots_dev, PLANES, rows, width)
        + vmem(ranks, rows, width)
        + vmem(ranks, rows, width)
        + vmem(slabs, rows, width)
        + [pltpu.VMEM((spots, 8, 128), jnp.float32)]
        + [pltpu.VMEM((8, 128), jnp.float32)]
        + [pltpu.VMEM((4, 8, 128), jnp.float32)]
        + [pltpu.VMEM((8, 128), jnp.float32)]
        + [sem((CHUNKS,))] * 10
        + [sem((3 * CHUNKS,))]
        + [sem((CHUNKS,)), sem((CHUNKS,)), sem(()), sem(()), sem((3,)), sem((3,)), sem(()), sem(()), sem(())]
    )
    vm = pl.BlockSpec(memory_space=pltpu.VMEM)
    anyspace = pl.BlockSpec(memory_space=pl.ANY)
    bf16 = jnp.bfloat16
    return pl.pallas_call(
        functools.partial(route_kernel, (shards, slabs, slots, ranks, inner, width)),
        out_shape=(
            jax.ShapeDtypeStruct(xs.shape, bf16),
            jax.ShapeDtypeStruct(xs.shape, bf16),
            jax.ShapeDtypeStruct(q.shape, bf16),
            jax.ShapeDtypeStruct((spots, 8, 128), jnp.float32),
        ),
        in_specs=[pl.BlockSpec(memory_space=pltpu.SMEM), vm, vm, vm, vm],
        out_specs=(anyspace, anyspace, anyspace, anyspace),
        scratch_shapes=scratch,
        compiler_params=pltpu.CompilerParams(collective_id=0, has_side_effects=True),
    )(tabs, xs, xo, q, part)


def tables(slab_owner, shards, inner, capacity, plane_here, spot_here):
    slabs = slab_owner.shape[0]
    slots = shards // PLANES * capacity
    ranks = slabs * 3 // 4
    ids = jnp.arange(slabs, dtype=jnp.int32)
    plane, spot = place(slab_owner, inner)
    earlier = ids[None, :] < ids[:, None]
    count = lambda mask: jnp.sum((mask & earlier).astype(jnp.int32), axis=1)
    slot = spot * capacity + count(slab_owner[:, None] == slab_owner[None, :])
    rank = count(plane[:, None] == plane[None, :])
    mine = plane == plane_here
    pick = lambda hit, value: jnp.sum(jnp.where(hit, value[None, :], 0), axis=1)
    at_slot = mine[None, :] & (slot[None, :] == jnp.arange(slots, dtype=jnp.int32)[:, None])
    at_rank = rank[None, :] == jnp.arange(ranks, dtype=jnp.int32)[:, None]
    tabs = jnp.concatenate(
        [
            pick(at_slot, ids),
            pick(at_slot, rank),
            pick(at_rank & ~mine[None, :], ids),
            pick(at_rank & mine[None, :], slot),
            mine.astype(jnp.int32),
            jnp.where(mine, slot, rank),
        ]
    )
    here = spot_here * capacity + jnp.arange(capacity, dtype=jnp.int32)
    used = jnp.any(mine[None, :] & (slot[None, :] == here[:, None]), axis=1)
    return tabs, mine, used


def nesterov(anchor_value, moment, mean_value):
    outer_grad = anchor_value - mean_value
    new_moment = MOMENTUM_COEF * moment + outer_grad
    new_anchor = anchor_value - OUTER_RATE * (outer_grad + MOMENTUM_COEF * new_moment)
    return (new_anchor, new_moment)


def on_device(
    replica_weights,
    anchor_slabs,
    momentum_slabs,
    slab_owner,
    replica_embed,
    anchor_embed,
    momentum_embed,
    embed_basis,
):
    rows = replica_weights[0]
    slabs, row_count, width = rows.shape
    half = width // 2
    shards = lax.axis_size("shard")
    n_group = lax.axis_size("group")
    inner = INNER[shards]
    lines = shards // PLANES // inner
    capacity = anchor_slabs.shape[1]
    anchor, moment = anchor_slabs[0], momentum_slabs[0]
    group = lax.axis_index("group")
    plane_here, spot_here = place(lax.axis_index("shard"), inner)
    tabs, mine, used = tables(slab_owner, shards, inner, capacity, plane_here, spot_here)

    keep_left = (mine == (group == 0))[:, None, None]
    left, right = rows[:, :, :half], rows[:, :, half:]
    xo = jnp.where(keep_left, left, right)
    xs = jnp.where(keep_left, right, left)
    q = ((1.0 - GRAD_COEF) * anchor - MOMENT_COEF * moment).astype(jnp.bfloat16)
    q = q.reshape(capacity, lines, PLANES, inner, row_count, half)

    embed_here = replica_embed[0].astype(jnp.float32)
    partial_factor = jnp.dot(
        embed_basis.T,
        anchor_embed / n_group - embed_here / n_group,
        precision=lax.Precision.HIGHEST,
    )
    part = partial_factor.reshape(shards // PLANES, 8, 128)

    near, far, sums, factor = route(tabs, xs, xo, q, part)

    new_rows = jnp.concatenate([jnp.where(keep_left, near, far), jnp.where(keep_left, far, near)], axis=2)
    summed = sums.reshape(anchor.shape).astype(jnp.float32)
    new_anchor, new_moment = nesterov(anchor, moment, summed / n_group)
    keep = used[:, None, None]
    new_anchor = jnp.where(keep, new_anchor, anchor)
    new_moment = jnp.where(keep, new_moment, moment)

    embed_factor = factor.reshape(partial_factor.shape)
    embed_grad = jnp.dot(embed_basis, embed_factor, precision=lax.Precision.HIGHEST)
    new_anchor_embed, new_momentum_embed = nesterov(
        anchor_embed, momentum_embed, anchor_embed - embed_grad
    )
    new_embed_rows = new_anchor_embed.astype(jnp.bfloat16)
    return (
        new_anchor[None],
        new_moment[None],
        new_rows[None],
        new_anchor_embed,
        new_momentum_embed,
        new_embed_rows[None],
    )


def solution(mesh):
    in_specs = (
        P("group", None, "shard", None),
        P("shard", None, None, "group"),
        P("shard", None, None, "group"),
        P(),
        P("group", "shard", None),
        P("shard", None),
        P("shard", None),
        P("shard", None),
    )
    out_specs = (
        P("shard", None, None, "group"),
        P("shard", None, None, "group"),
        P("group", None, "shard", None),
        P("shard", None),
        P("shard", None),
        P("group", "shard", None),
    )
    return jax.shard_map(
        on_device, mesh=mesh, in_specs=in_specs, out_specs=out_specs, check_vma=False
    )
```

```python
import functools

import jax
import jax.numpy as jnp
from jax import lax
from jax.experimental import pallas as pl
from jax.experimental.pallas import tpu as pltpu
from jax.sharding import PartitionSpec as P

OUTER_RATE = 0.7
MOMENTUM_COEF = 0.9
GRAD_COEF = OUTER_RATE * (1.0 + MOMENTUM_COEF)
MOMENT_COEF = OUTER_RATE * MOMENTUM_COEF * MOMENTUM_COEF
PLANES = 2
INNER = {64: 8, 8: 2}
CHUNKS = 4
UNROLL = 4
MESH = pl.DeviceIdType.MESH


def place(shard, inner):
    plane = lax.rem(lax.div(shard, inner), PLANES)
    spot = lax.div(shard, PLANES * inner) * inner + lax.rem(shard, inner)
    return plane, spot


def shard_of(spot, plane, inner):
    return lax.div(spot, inner) * (PLANES * inner) + plane * inner + lax.rem(spot, inner)


def loop(count, body):
    unroll = UNROLL if count % UNROLL == 0 else 1

    def step(i, carry):
        for u in range(unroll):
            body(i * unroll + u)
        return carry

    lax.fori_loop(0, count // unroll, step, 0)


def each(start, stop, body):
    def step(i, carry):
        body(i)
        return carry

    lax.fori_loop(start, stop, step, 0)


def route_kernel(sizes, tabs, x, a, m, basis, embed, anchor_embed, na, nm, w_out, e_out, *scratch):
    shards, slabs, slots, ranks, inner, width = sizes
    chunks = CHUNKS
    spots = shards // PLANES
    capacity = slots // spots
    half = width * chunks
    bf16, f32 = jnp.bfloat16, jnp.float32
    (xl, xr, xs, xo, r, s, fc, cf, ys, fr, qb, qr, qc, qd, nn, nr) = [
        scratch[i * chunks : (i + 1) * chunks] for i in range(16)
    ]
    part, er, e1, ex, e2, *sems = scratch[16 * chunks :]
    (sa, ra, sc, rc, sq, rq, sd, rd, sf, rf, sn, rn, lx, ly, la, lm, lq, lf) = sems[:18]
    (se, re, sx, rx, sg, rg, le) = sems[18:]

    group = lax.axis_index("group")
    shard = lax.axis_index("shard")
    plane, spot = place(shard, inner)
    line, lane = lax.div(spot, inner), lax.rem(spot, inner)
    other = 1 - plane
    partner = (1 - group, shard)
    across = (1 - group, shard_of(spot, other, inner))
    corner = (group, shard_of(spot, other, inner))

    def peer(i):
        d = lax.rem(spot + i, spots)
        return d, (group, shard_of(d, plane, inner))

    def remote(src, dst, send, recv, device):
        return pltpu.make_async_remote_copy(
            src_ref=src, dst_ref=dst, send_sem=send, recv_sem=recv, device_id=device, device_id_type=MESH
        )

    def drain(ref, sem):
        pltpu.make_async_copy(ref, ref, sem).wait()

    off_fo, off_rk = 0, slots
    off_fc, off_fp = 2 * slots, 2 * slots + ranks
    off_in, off_ts = 2 * slots + 2 * ranks, 2 * slots + 2 * ranks + slabs
    off_used = off_ts + slabs

    def cols(k):
        return pl.ds(k * width, width)

    def right(k):
        return pl.ds(half + k * width, width)

    for k in range(chunks):
        pltpu.make_async_copy(x.at[:, :, cols(k)], xl[k], lx.at[k]).start()
        pltpu.make_async_copy(x.at[:, :, right(k)], xr[k], ly.at[k]).start()
        pltpu.make_async_copy(a.at[:, :, :, cols(k)], na.at[:, :, :, cols(k)], la.at[k]).start()
        pltpu.make_async_copy(m.at[:, :, :, cols(k)], nm.at[:, :, :, cols(k)], lm.at[k]).start()

    barrier = pltpu.get_barrier_semaphore()

    def greet(i):
        pl.semaphore_signal(barrier, inc=1, device_id=peer(i)[1], device_id_type=MESH)

    each(1, spots, greet)
    for device in (partner, across, corner):
        pl.semaphore_signal(barrier, inc=1, device_id=device, device_id_type=MESH)
    pl.semaphore_wait(barrier, spots - 1 + 3)

    def is_left(t):
        return lax.rem(tabs[off_in + t] + group, 2) == 1

    def start_x(k):
        drain(xl[k], lx.at[k])
        drain(xr[k], ly.at[k])

        def split(t):
            left = is_left(t)
            one, two = xl[k][t], xr[k][t]
            xs[k][t] = jnp.where(left, two, one)
            xo[k][t] = jnp.where(left, one, two)

        loop(slabs, split)
        remote(xs[k], r[k], sa.at[k], ra.at[k], partner).start()

    def start_q(k):
        drain(na.at[:, :, :, cols(k)], la.at[k])
        drain(nm.at[:, :, :, cols(k)], lm.at[k])

        def base(n):
            z, b, i = lax.div(n, PLANES * inner), lax.rem(lax.div(n, inner), PLANES), lax.rem(n, inner)
            for c in range(capacity):
                value = (1.0 - GRAD_COEF) * na[c, n, :, cols(k)] - MOMENT_COEF * nm[c, n, :, cols(k)]
                qb[k][c, z, b, i] = value.astype(bf16)

        loop(shards, base)

        def send_q(i):
            d, device = peer(i)
            remote(
                qb[k].at[:, lax.div(d, inner), :, lax.rem(d, inner)], qr[k].at[spot], sq.at[k], rq.at[k], device
            ).start()

        each(1, spots, send_q)
        pltpu.make_async_copy(qb[k].at[:, line, :, lane], qr[k].at[spot], lq.at[k]).start()

    def tile(ref, d):
        per = ref.shape[1] // 128
        return ref.at[pl.ds(lax.div(d, per) * 8, 8), pl.ds(pl.multiple_of(lax.rem(d, per) * 128, 128), 128)]

    def factor_start():
        diff = 0.5 * anchor_embed[...] - 0.5 * embed[...].astype(f32)
        part[...] = lax.dot_general(
            basis[...], diff, (((0,), (0,)), ((), ())), precision=lax.Precision.HIGHEST, preferred_element_type=f32
        )

        def send_part(i):
            d, device = peer(i)
            remote(tile(part, d), er.at[spot], se, re, device).start()

        each(1, spots, send_part)
        er[spot] = tile(part, spot)[...]

    def stage_sum(k):
        drain(r[k], ra.at[k])

        def add(t):
            both = xo[k][t].astype(f32) + r[k][t].astype(f32)
            s[k][t] = both.astype(bf16)

        loop(slabs, add)

        def pick_cross(i):
            fc[k][i] = s[k][tabs[off_fc + i]]

        loop(ranks, pick_cross)
        remote(fc[k], cf[k], sc.at[k], rc.at[k], across).start()

        def pick_own(j):
            ys[k][lax.div(j, capacity), lax.rem(j, capacity), plane] = s[k][tabs[off_fo + j]]

        loop(slots, pick_own)

    def stage_q(k):
        drain(qr[k].at[pl.ds(0, spots - 1)], rq.at[k])
        drain(qr[k].at[0], lq.at[k])

        def pick(i):
            j = tabs[off_fp + i]
            qc[k][i] = qr[k][lax.div(j, capacity), lax.rem(j, capacity), other]

        loop(ranks, pick)
        remote(qc[k], qd[k], sd.at[k], rd.at[k], across).start()

    def stage_route(k):
        drain(cf[k], rc.at[k])

        def pick(j):
            ys[k][lax.div(j, capacity), lax.rem(j, capacity), other] = cf[k][tabs[off_rk + j]]

        loop(slots, pick)

        def send(i):
            d, device = peer(i)
            remote(ys[k].at[d], fr[k].at[:, line, :, lane], sf.at[k], rf.at[k], device).start()

        each(1, spots, send)
        pltpu.make_async_copy(ys[k].at[spot], fr[k].at[:, line, :, lane], lf.at[k]).start()

    def stage_new(k):
        drain(qd[k], rd.at[k])

        def combine(t):
            own = tabs[off_in + t]
            where = tabs[off_ts + t]
            j = where * own
            here = qr[k][lax.div(j, capacity), lax.rem(j, capacity), plane]
            there = qd[k][where * (1 - own)]
            base = jnp.where(own == 1, here.astype(f32), there.astype(f32))
            new = base + (0.5 * GRAD_COEF) * s[k][t].astype(f32)
            nn[k][t] = new.astype(bf16)

        loop(slabs, combine)
        remote(nn[k], nr[k], sn.at[k], rn.at[k], partner).start()

    def finish_owned(k):
        drain(qr[k].at[pl.ds(0, spots - 1)], rf.at[k])
        drain(qr[k].at[0], lf.at[k])

        def step(n):
            z, b, i = lax.div(n, PLANES * inner), lax.rem(lax.div(n, inner), PLANES), lax.rem(n, inner)
            for c in range(capacity):
                used = tabs[off_used + c] == 1
                anchor, moment = na[c, n, :, cols(k)], nm[c, n, :, cols(k)]
                new_anchor, new_moment = nesterov(anchor, moment, 0.5 * fr[k][c, z, b, i].astype(f32))
                na[c, n, :, cols(k)] = jnp.where(used, new_anchor, anchor)
                nm[c, n, :, cols(k)] = jnp.where(used, new_moment, moment)

        loop(shards, step)

    def finish_weights(k):
        drain(nr[k], rn.at[k])

        def merge(t):
            left = is_left(t)
            near, far = nn[k][t], nr[k][t]
            w_out[t, :, cols(k)] = jnp.where(left, near, far)
            w_out[t, :, right(k)] = jnp.where(left, far, near)

        loop(slabs, merge)

    def factor_sum():
        drain(er.at[pl.ds(0, spots - 1)], re)
        e1[...] = jnp.sum(er[...], axis=0)
        at = PLANES * plane + group
        ex[at] = e1[...]
        for n, device in enumerate((partner, across, corner)):
            remote(e1, ex.at[at], sx.at[n], rx.at[n], device).start()

    def factor_send():
        for n in range(3):
            drain(e1, rx.at[n])
        e2[...] = jnp.sum(ex[...], axis=0)

        def send(i):
            remote(e2, tile(e_out, spot), sg, rg, peer(i)[1]).start()

        each(1, spots, send)
        pltpu.make_async_copy(e2, tile(e_out, spot), le).start()

    for k in range(chunks):
        start_x(k)
        start_q(k)
        if k == 0:
            factor_start()
    for k in range(chunks):
        stage_sum(k)
        stage_q(k)
        if k == 0:
            factor_sum()
        if k == 1:
            factor_send()
        if k >= 1:
            stage_route(k - 1)
            stage_new(k - 1)
    stage_route(chunks - 1)
    stage_new(chunks - 1)
    for k in range(chunks):
        finish_weights(k)
        finish_owned(k)

    for k in range(chunks):
        some = qr[k].at[pl.ds(0, spots - 1)]
        drain(r[k], sa.at[k])
        drain(cf[k], sc.at[k])
        drain(qd[k], sd.at[k])
        drain(some, sq.at[k])
        drain(some, sf.at[k])
        drain(nn[k], sn.at[k])
    for n in range(3):
        drain(e1, sx.at[n])
    drain(er.at[pl.ds(0, spots - 1)], se)
    drain(er.at[pl.ds(0, spots - 1)], sg)
    drain(er.at[pl.ds(0, spots - 1)], rg)
    drain(e2, le)


def route(tabs, x, a, m, basis, embed, anchor_embed, inner):
    slabs, rows, full = x.shape
    capacity, shards, _, half = a.shape
    spots = shards // PLANES
    lines = spots // inner
    slots = spots * capacity
    ranks = slabs * 3 // 4
    width = half // CHUNKS
    bf16, f32 = jnp.bfloat16, jnp.float32
    vmem = lambda *shape: [pltpu.VMEM(shape, bf16)] * CHUNKS
    sem = pltpu.SemaphoreType.DMA
    whole = (slabs, rows, width)
    most = (ranks, rows, width)
    spread = (spots, capacity, PLANES, rows, width)
    laid = (capacity, lines, PLANES, inner, rows, width)
    factor = (basis.shape[1], embed.shape[1])
    scratch = []
    for shape in (whole,) * 6 + (most, most, spread, laid, laid, spread, most, most, whole, whole):
        scratch += vmem(*shape)
    scratch += [
        pltpu.VMEM(factor, f32),
        pltpu.VMEM((spots, 8, 128), f32),
        pltpu.VMEM((8, 128), f32),
        pltpu.VMEM((4, 8, 128), f32),
        pltpu.VMEM((8, 128), f32),
    ]
    scratch += [sem((CHUNKS,))] * 18
    scratch += [sem(()), sem(()), sem((3,)), sem((3,)), sem(()), sem(()), sem(())]
    vm = pl.BlockSpec(memory_space=pltpu.VMEM)
    hbm = pl.BlockSpec(memory_space=pltpu.HBM)
    keep = lambda array: pltpu.with_memory_space_constraint(array, pltpu.HBM)
    return pl.pallas_call(
        functools.partial(route_kernel, (shards, slabs, slots, ranks, inner, width)),
        out_shape=(
            pltpu.VMEM(a.shape, f32),
            pltpu.VMEM(a.shape, f32),
            pltpu.VMEM(x.shape, bf16),
            pltpu.HBM(factor, f32),
        ),
        in_specs=[pl.BlockSpec(memory_space=pltpu.SMEM), hbm, hbm, hbm, vm, vm, vm],
        out_specs=(vm, vm, vm, hbm),
        scratch_shapes=scratch,
        compiler_params=pltpu.CompilerParams(collective_id=0, has_side_effects=True, vmem_limit_bytes=30 << 20),
    )(tabs, keep(x), keep(a), keep(m), basis, embed, anchor_embed)


def tables(slab_owner, shards, inner, capacity, plane_here, spot_here):
    slabs = slab_owner.shape[0]
    slots = shards // PLANES * capacity
    ranks = slabs * 3 // 4
    ids = jnp.arange(slabs, dtype=jnp.int32)
    plane, spot = place(slab_owner, inner)
    earlier = ids[None, :] < ids[:, None]
    count = lambda mask: jnp.sum((mask & earlier).astype(jnp.int32), axis=1)
    slot = spot * capacity + count(slab_owner[:, None] == slab_owner[None, :])
    rank = count(plane[:, None] == plane[None, :])
    mine = plane == plane_here
    pick = lambda hit, value: jnp.sum(jnp.where(hit, value[None, :], 0), axis=1)
    at_slot = mine[None, :] & (slot[None, :] == jnp.arange(slots, dtype=jnp.int32)[:, None])
    at_rank = rank[None, :] == jnp.arange(ranks, dtype=jnp.int32)[:, None]
    here = spot_here * capacity + jnp.arange(capacity, dtype=jnp.int32)
    used = jnp.any(mine[None, :] & (slot[None, :] == here[:, None]), axis=1)
    tabs = jnp.concatenate(
        [
            pick(at_slot, ids),
            pick(at_slot, rank),
            pick(at_rank & ~mine[None, :], ids),
            pick(at_rank & mine[None, :], slot),
            mine.astype(jnp.int32),
            jnp.where(mine, slot, rank),
            used.astype(jnp.int32),
        ]
    )
    return tabs


def nesterov(anchor_value, moment, mean_value):
    outer_grad = anchor_value - mean_value
    new_moment = MOMENTUM_COEF * moment + outer_grad
    new_anchor = anchor_value - OUTER_RATE * (outer_grad + MOMENTUM_COEF * new_moment)
    return (new_anchor, new_moment)


def on_device(
    replica_weights,
    anchor_slabs,
    momentum_slabs,
    slab_owner,
    replica_embed,
    anchor_embed,
    momentum_embed,
    embed_basis,
):
    rows = replica_weights[0]
    slabs, row_count, width = rows.shape
    half = width // 2
    shards = lax.axis_size("shard")
    inner = INNER[shards]
    capacity = anchor_slabs.shape[1]
    anchor, moment = anchor_slabs[0], momentum_slabs[0]
    plane_here, spot_here = place(lax.axis_index("shard"), inner)
    tabs = tables(slab_owner, shards, inner, capacity, plane_here, spot_here)
    by_rows = lambda slab: slab.reshape(capacity, shards, row_count, half)
    new_anchor, new_moment, new_rows, embed_factor = route(
        tabs, rows, by_rows(anchor), by_rows(moment), embed_basis, replica_embed[0], anchor_embed, inner
    )
    new_anchor, new_moment = new_anchor.reshape(anchor.shape), new_moment.reshape(anchor.shape)
    embed_grad = jnp.dot(embed_basis, embed_factor, precision=lax.Precision.HIGHEST)
    new_anchor_embed, new_momentum_embed = nesterov(
        anchor_embed, momentum_embed, anchor_embed - embed_grad
    )
    new_embed_rows = new_anchor_embed.astype(jnp.bfloat16)
    return (
        new_anchor[None],
        new_moment[None],
        new_rows[None],
        new_anchor_embed,
        new_momentum_embed,
        new_embed_rows[None],
    )


def solution(mesh):
    in_specs = (
        P("group", None, "shard", None),
        P("shard", None, None, "group"),
        P("shard", None, None, "group"),
        P(),
        P("group", "shard", None),
        P("shard", None),
        P("shard", None),
        P("shard", None),
    )
    out_specs = (
        P("shard", None, None, "group"),
        P("shard", None, None, "group"),
        P("group", None, "shard", None),
        P("shard", None),
        P("shard", None),
        P("group", "shard", None),
    )
    return jax.shard_map(
        on_device, mesh=mesh, in_specs=in_specs, out_specs=out_specs, check_vma=False
    )
```

```python
import functools

import jax
import jax.numpy as jnp
from jax import lax
from jax.experimental import pallas as pl
from jax.experimental.pallas import tpu as pltpu
from jax.sharding import PartitionSpec as P

OUTER_RATE = 0.7
MOMENTUM_COEF = 0.9
GRAD_COEF = OUTER_RATE * (1.0 + MOMENTUM_COEF)
MOMENT_COEF = OUTER_RATE * MOMENTUM_COEF * MOMENTUM_COEF
PLANES = 2
INNER = {64: 8, 8: 2}
PIECES = (2, 2, 2, 1, 1)
CHUNKS = len(PIECES)
UNROLL = 4
MESH = pl.DeviceIdType.MESH


def place(shard, inner):
    plane = lax.rem(lax.div(shard, inner), PLANES)
    spot = lax.div(shard, PLANES * inner) * inner + lax.rem(shard, inner)
    return plane, spot


def shard_of(spot, plane, inner):
    return lax.div(spot, inner) * (PLANES * inner) + plane * inner + lax.rem(spot, inner)


def cuts(half):
    unit = half // sum(PIECES)
    return [unit * sum(PIECES[:k]) for k in range(CHUNKS)], [unit * piece for piece in PIECES]


def loop(count, body):
    unroll = UNROLL if count % UNROLL == 0 else 1

    def step(i, carry):
        for u in range(unroll):
            body(i * unroll + u)
        return carry

    lax.fori_loop(0, count // unroll, step, 0)


def each(start, stop, body):
    def step(i, carry):
        body(i)
        return carry

    lax.fori_loop(start, stop, step, 0)


def route_kernel(sizes, owners, x, a, m, basis_in, embed_in, anchor_in, na, nm, w_out, e_out, *scratch):
    shards, slabs, slots, ranks, inner, half = sizes
    starts, widths = cuts(half)
    chunks = CHUNKS
    spots = shards // PLANES
    capacity = slots // spots
    bf16, f32 = jnp.bfloat16, jnp.float32
    (xl, xr, xs, xo, r, s, fc, cf, ys, fr, qb, qr, qc, qd, nn, nr) = [
        scratch[i * chunks : (i + 1) * chunks] for i in range(16)
    ]
    part, er, e1, ex, e2, basis, embed, anchor_embed, column, rows_v, tabs, *sems = scratch[16 * chunks :]
    (sa, ra, sc, rc, sq, rq, sd, rd, sf, rf, sn, rn, lx, ly, la, lm, lq, lf) = sems[:18]
    (se, re, sx, rx, sg, rg, le, lt, li) = sems[18:]

    group = lax.axis_index("group")
    shard = lax.axis_index("shard")
    plane, spot = place(shard, inner)
    other = 1 - plane
    partner = (1 - group, shard)
    across = (1 - group, shard_of(spot, other, inner))
    corner = (group, shard_of(spot, other, inner))

    def peer(i):
        d = lax.rem(spot + i, spots)
        return d, (group, shard_of(d, plane, inner))

    def remote(src, dst, send, recv, device):
        return pltpu.make_async_remote_copy(
            src_ref=src, dst_ref=dst, send_sem=send, recv_sem=recv, device_id=device, device_id_type=MESH
        )

    def drain(ref, sem):
        pltpu.make_async_copy(ref, ref, sem).wait()

    def cols(k):
        return pl.ds(starts[k], widths[k])

    def right(k):
        return pl.ds(half + starts[k], widths[k])

    small = ((basis_in, basis), (embed_in, embed), (anchor_in, anchor_embed))
    for k in range(chunks):
        pltpu.make_async_copy(x.at[:, :, cols(k)], xl[k], lx.at[k]).start()
        pltpu.make_async_copy(x.at[:, :, right(k)], xr[k], ly.at[k]).start()
        if k == 0:
            for n, (src, dst) in enumerate(small):
                pltpu.make_async_copy(src, dst, li.at[n]).start()
        pltpu.make_async_copy(a.at[:, :, :, cols(k)], na.at[:, :, :, cols(k)], la.at[k]).start()
        pltpu.make_async_copy(m.at[:, :, :, cols(k)], nm.at[:, :, :, cols(k)], lm.at[k]).start()

    barrier = pltpu.get_barrier_semaphore()

    def greet(i):
        pl.semaphore_signal(barrier, inc=1, device_id=peer(i)[1], device_id_type=MESH)

    each(1, spots, greet)
    for device in (partner, across, corner):
        pl.semaphore_signal(barrier, inc=1, device_id=device, device_id_type=MESH)
    pl.semaphore_wait(barrier, spots - 1 + 3)

    def is_left(t):
        return (place(owners[t], inner)[0] == plane) == (group == 0)

    FO, RK, FC, FP, IN, TS, USED = range(7)

    def fill_tables():
        def put(t):
            column[pl.ds(t, 1), :] = jnp.full((1, 128), owners[t], jnp.int32)

        loop(slabs, put)
        owner = column[...]
        sub = lax.broadcasted_iota(jnp.int32, owner.shape, 0)
        at = lax.broadcasted_iota(jnp.int32, owner.shape, 1)
        down = lambda hit, value: jnp.sum(jnp.where(hit, value, 0), axis=0, keepdims=True)
        count = lambda hit: jnp.sum(jnp.where(hit & (at < sub), 1, 0), axis=1, keepdims=True)
        own_plane, own_spot = place(owner, inner)
        row = down(at == sub, owner)
        row_plane = place(row, inner)[0]
        slot = own_spot * capacity + count(owner == row)
        rank = jnp.broadcast_to(count(own_plane == row_plane), owner.shape)
        mine = own_plane == plane
        rows_v[pl.ds(FO, 1), :] = jnp.minimum(down(mine & (slot == at), sub), slabs - 1)
        rows_v[pl.ds(RK, 1), :] = jnp.minimum(down(mine & (slot == at), rank), ranks - 1)
        rows_v[pl.ds(FC, 1), :] = jnp.minimum(down((own_plane != plane) & (rank == at), sub), slabs - 1)
        rows_v[pl.ds(FP, 1), :] = jnp.minimum(down(mine & (rank == at), slot), slots - 1)
        rows_v[pl.ds(IN, 1), :] = down(mine & (at == sub), 1)
        rows_v[pl.ds(TS, 1), :] = down(at == sub, jnp.where(mine, jnp.minimum(slot, slots - 1), jnp.minimum(rank, ranks - 1)))
        rows_v[pl.ds(USED, 1), :] = down(mine & (slot == at), 1)
        pltpu.make_async_copy(rows_v, tabs, lt).start()
        drain(tabs, lt)

    def start_x(k):
        drain(xl[k], lx.at[k])
        drain(xr[k], ly.at[k])

        def split(t):
            left = is_left(t)
            one, two = xl[k][t], xr[k][t]
            xs[k][t] = jnp.where(left, two, one)
            xo[k][t] = jnp.where(left, one, two)

        loop(slabs, split)
        remote(xs[k], r[k], sa.at[k], ra.at[k], partner).start()

    def start_q(k):
        drain(na.at[:, :, :, cols(k)], la.at[k])
        drain(nm.at[:, :, :, cols(k)], lm.at[k])

        def base(n):
            z, b, i = lax.div(n, PLANES * inner), lax.rem(lax.div(n, inner), PLANES), lax.rem(n, inner)
            for c in range(capacity):
                value = (1.0 - GRAD_COEF) * na[c, n, :, cols(k)] - MOMENT_COEF * nm[c, n, :, cols(k)]
                qb[k][z * inner + i, c, b] = value.astype(bf16)

        loop(shards, base)

        def send_q(i):
            d, device = peer(i)
            remote(
                qb[k].at[d], qr[k].at[spot], sq.at[k], rq.at[k], device
            ).start()

        each(1, spots, send_q)
        pltpu.make_async_copy(qb[k].at[spot], qr[k].at[spot], lq.at[k]).start()

    def tile(ref, d):
        per = ref.shape[1] // 128
        return ref.at[pl.ds(lax.div(d, per) * 8, 8), pl.ds(pl.multiple_of(lax.rem(d, per) * 128, 128), 128)]

    def factor_start():
        for n, (_, dst) in enumerate(small):
            drain(dst, li.at[n])
        diff = 0.5 * anchor_embed[...] - 0.5 * embed[...].astype(f32)
        part[...] = lax.dot_general(
            basis[...], diff, (((0,), (0,)), ((), ())), precision=lax.Precision.HIGHEST, preferred_element_type=f32
        )

        def send_part(i):
            d, device = peer(i)
            remote(tile(part, d), er.at[spot], se, re, device).start()

        each(1, spots, send_part)
        er[spot] = tile(part, spot)[...]

    def stage_sum(k):
        drain(r[k], ra.at[k])

        def add(t):
            both = xo[k][t].astype(f32) + r[k][t].astype(f32)
            s[k][t] = both.astype(bf16)

        loop(slabs, add)

        def pick_cross(i):
            fc[k][i] = s[k][tabs[FC, i]]

        loop(ranks, pick_cross)
        remote(fc[k], cf[k], sc.at[k], rc.at[k], across).start()

        def pick_own(j):
            ys[k][lax.div(j, capacity), lax.rem(j, capacity), plane] = s[k][tabs[FO, j]]

        loop(slots, pick_own)

    def stage_q(k):
        drain(qr[k].at[pl.ds(0, spots - 1)], rq.at[k])
        drain(qr[k].at[0], lq.at[k])

        def pick(i):
            j = tabs[FP, i]
            qc[k][i] = qr[k][lax.div(j, capacity), lax.rem(j, capacity), other]

        loop(ranks, pick)
        remote(qc[k], qd[k], sd.at[k], rd.at[k], across).start()

    def stage_route(k):
        drain(cf[k], rc.at[k])

        def pick(j):
            ys[k][lax.div(j, capacity), lax.rem(j, capacity), other] = cf[k][tabs[RK, j]]

        loop(slots, pick)

        def send(i):
            d, device = peer(i)
            remote(ys[k].at[d], fr[k].at[spot], sf.at[k], rf.at[k], device).start()

        each(1, spots, send)
        pltpu.make_async_copy(ys[k].at[spot], fr[k].at[spot], lf.at[k]).start()

    def stage_new(k):
        drain(qd[k], rd.at[k])

        def combine(t):
            own = tabs[IN, t]
            where = tabs[TS, t]
            j = where * own
            here = qr[k][lax.div(j, capacity), lax.rem(j, capacity), plane]
            there = qd[k][where * (1 - own)]
            base = jnp.where(own == 1, here.astype(f32), there.astype(f32))
            new = base + (0.5 * GRAD_COEF) * s[k][t].astype(f32)
            nn[k][t] = new.astype(bf16)

        loop(slabs, combine)
        remote(nn[k], nr[k], sn.at[k], rn.at[k], partner).start()

    def finish_owned(k):
        drain(qr[k].at[pl.ds(0, spots - 1)], rf.at[k])
        drain(qr[k].at[0], lf.at[k])

        def step(n):
            z, b, i = lax.div(n, PLANES * inner), lax.rem(lax.div(n, inner), PLANES), lax.rem(n, inner)
            for c in range(capacity):
                used = tabs[USED, spot * capacity + c] == 1
                anchor, moment = na[c, n, :, cols(k)], nm[c, n, :, cols(k)]
                new_anchor, new_moment = nesterov(anchor, moment, 0.5 * fr[k][z * inner + i, c, b].astype(f32))
                na[c, n, :, cols(k)] = jnp.where(used, new_anchor, anchor)
                nm[c, n, :, cols(k)] = jnp.where(used, new_moment, moment)

        loop(shards, step)

    def finish_weights(k):
        drain(nr[k], rn.at[k])

        def merge(t):
            left = is_left(t)
            near, far = nn[k][t], nr[k][t]
            w_out[t, :, cols(k)] = jnp.where(left, near, far)
            w_out[t, :, right(k)] = jnp.where(left, far, near)

        loop(slabs, merge)

    def factor_sum():
        drain(er.at[pl.ds(0, spots - 1)], re)
        e1[...] = jnp.sum(er[...], axis=0)
        at = PLANES * plane + group
        ex[at] = e1[...]
        for n, device in enumerate((partner, across, corner)):
            remote(e1, ex.at[at], sx.at[n], rx.at[n], device).start()

    def factor_send():
        for n in range(3):
            drain(e1, rx.at[n])
        e2[...] = jnp.sum(ex[...], axis=0)

        def send(i):
            remote(e2, tile(e_out, spot), sg, rg, peer(i)[1]).start()

        each(1, spots, send)
        pltpu.make_async_copy(e2, tile(e_out, spot), le).start()

    for k in range(chunks):
        start_x(k)
        start_q(k)
        if k == 0:
            factor_start()
    fill_tables()
    for k in range(chunks):
        stage_sum(k)
        stage_q(k)
        if k == 0:
            factor_sum()
        if k == 1:
            factor_send()
        if k >= 1:
            stage_route(k - 1)
            stage_new(k - 1)
    stage_route(chunks - 1)
    stage_new(chunks - 1)
    for k in range(chunks):
        finish_weights(k)
        finish_owned(k)

    for k in range(chunks):
        some = qr[k].at[pl.ds(0, spots - 1)]
        drain(r[k], sa.at[k])
        drain(cf[k], sc.at[k])
        drain(qd[k], sd.at[k])
        drain(some, sq.at[k])
        drain(some, sf.at[k])
        drain(nn[k], sn.at[k])
    for n in range(3):
        drain(e1, sx.at[n])
    drain(er.at[pl.ds(0, spots - 1)], se)
    drain(er.at[pl.ds(0, spots - 1)], sg)
    drain(er.at[pl.ds(0, spots - 1)], rg)
    drain(e2, le)


def route(owners, x, a, m, basis, embed, anchor_embed, inner):
    slabs, rows, full = x.shape
    capacity, shards, _, half = a.shape
    spots = shards // PLANES
    slots = spots * capacity
    ranks = slabs * 3 // 4
    bf16, f32 = jnp.bfloat16, jnp.float32
    sem = pltpu.SemaphoreType.DMA
    whole = (slabs, rows)
    most = (ranks, rows)
    spread = (spots, capacity, PLANES, rows)
    factor = (basis.shape[1], embed.shape[1])
    scratch = []
    for shape in (whole,) * 6 + (most, most, spread, spread, spread, spread, most, most, whole, whole):
        scratch += [pltpu.VMEM((*shape, width), bf16) for width in cuts(half)[1]]
    scratch += [
        pltpu.VMEM(factor, f32),
        pltpu.VMEM((spots, 8, 128), f32),
        pltpu.VMEM((8, 128), f32),
        pltpu.VMEM((4, 8, 128), f32),
        pltpu.VMEM((8, 128), f32),
        pltpu.VMEM(basis.shape, f32),
        pltpu.VMEM(embed.shape, bf16),
        pltpu.VMEM(anchor_embed.shape, f32),
        pltpu.VMEM((slabs, 128), jnp.int32),
        pltpu.VMEM((8, 128), jnp.int32),
        pltpu.SMEM((8, 128), jnp.int32),
    ]
    scratch += [sem((CHUNKS,))] * 18
    scratch += [sem(()), sem(()), sem((3,)), sem((3,)), sem(()), sem(()), sem(()), sem(()), sem((3,))]
    vm = pl.BlockSpec(memory_space=pltpu.VMEM)
    hbm = pl.BlockSpec(memory_space=pltpu.HBM)
    keep = lambda array: pltpu.with_memory_space_constraint(array, pltpu.HBM)
    return pl.pallas_call(
        functools.partial(route_kernel, (shards, slabs, slots, ranks, inner, half)),
        out_shape=(
            pltpu.VMEM(a.shape, f32),
            pltpu.VMEM(a.shape, f32),
            pltpu.VMEM(x.shape, bf16),
            pltpu.HBM(factor, f32),
        ),
        in_specs=[pl.BlockSpec(memory_space=pltpu.SMEM)] + [hbm] * 6,
        out_specs=(vm, vm, vm, hbm),
        scratch_shapes=scratch,
        compiler_params=pltpu.CompilerParams(collective_id=0, has_side_effects=True, vmem_limit_bytes=30 << 20),
    )(owners, *map(keep, (x, a, m, basis, embed, anchor_embed)))


def nesterov(anchor_value, moment, mean_value):
    outer_grad = anchor_value - mean_value
    new_moment = MOMENTUM_COEF * moment + outer_grad
    new_anchor = anchor_value - OUTER_RATE * (outer_grad + MOMENTUM_COEF * new_moment)
    return (new_anchor, new_moment)


def on_device(
    replica_weights,
    anchor_slabs,
    momentum_slabs,
    slab_owner,
    replica_embed,
    anchor_embed,
    momentum_embed,
    embed_basis,
):
    rows = replica_weights[0]
    slabs, row_count, width = rows.shape
    half = width // 2
    shards = lax.axis_size("shard")
    inner = INNER[shards]
    capacity = anchor_slabs.shape[1]
    anchor, moment = anchor_slabs[0], momentum_slabs[0]
    by_rows = lambda slab: slab.reshape(capacity, shards, row_count, half)
    new_anchor, new_moment, new_rows, embed_factor = route(
        slab_owner, rows, by_rows(anchor), by_rows(moment), embed_basis, replica_embed[0], anchor_embed, inner
    )
    new_anchor, new_moment = new_anchor.reshape(anchor.shape), new_moment.reshape(anchor.shape)
    embed_grad = jnp.dot(embed_basis, embed_factor, precision=lax.Precision.HIGHEST)
    new_anchor_embed, new_momentum_embed = nesterov(
        anchor_embed, momentum_embed, anchor_embed - embed_grad
    )
    new_embed_rows = new_anchor_embed.astype(jnp.bfloat16)
    return (
        new_anchor[None],
        new_moment[None],
        new_rows[None],
        new_anchor_embed,
        new_momentum_embed,
        new_embed_rows[None],
    )


def solution(mesh):
    in_specs = (
        P("group", None, "shard", None),
        P("shard", None, None, "group"),
        P("shard", None, None, "group"),
        P(),
        P("group", "shard", None),
        P("shard", None),
        P("shard", None),
        P("shard", None),
    )
    out_specs = (
        P("shard", None, None, "group"),
        P("shard", None, None, "group"),
        P("group", None, "shard", None),
        P("shard", None),
        P("shard", None),
        P("group", "shard", None),
    )
    return jax.shard_map(
        on_device, mesh=mesh, in_specs=in_specs, out_specs=out_specs, check_vma=False
    )
```
